32 devices in a mesh: dp: 8 (over z, core), tensor: 4 (over y, x).
Axes of the slice: x: 2, y: 2, z: 4, core: 2. Of those that a mesh axis runs over, the one named last changes fastest.
Arguments:
- layer_input: bfloat16 [16, 1024, 2048], P('dp', 'tensor'), may hold values from -6 to 6
- prefix_lengths: int32 [16], P('dp'), may hold values from 102 to 512
- gains: float32 [4352], P(('dp', 'tensor')), may hold values from 0.5 to 2.5
- w_query: bfloat16 [2048, 2048], P('dp', 'tensor'), may hold values from -0.125 to 0.125
- key_matrix: bfloat16 [2048, 1024], P('dp', 'tensor'), may hold values from -0.125 to 0.125
- value_matrix: bfloat16 [2048, 1024], P('dp', 'tensor'), may hold values from -0.125 to 0.125
- w_gate_head: bfloat16 [2048, 16], P('dp', 'tensor'), may hold values from -0.125 to 0.125
- w_output: bfloat16 [2048, 2048], P('tensor', 'dp'), may hold values from -1 to 1
- w_gate: bfloat16 [2048, 6144], P('dp', 'tensor'), may hold values from -0.125 to 0.125
- w_up: bfloat16 [2048, 6144], P('dp', 'tensor'), may hold values from -0.125 to 0.125
- w_down: bfloat16 [6144, 2048], P('tensor', 'dp'), may hold values from -0.078125 to 0.078125
- out_grad: bfloat16 [16, 1024, 2048], P('dp', 'tensor'), may hold values from -6 to 6
Outputs:
- block_output: bfloat16 [16, 1024, 2048], P('dp', 'tensor')
- input_grad: float32 [16, 1024, 2048], P('dp', 'tensor')
- gains_grad: float32 [4352], P(('dp', 'tensor'))
- w_query_grad: float32 [2048, 2048], P('dp', 'tensor')
- w_key_grad: float32 [2048, 1024], P('dp', 'tensor')
- w_value_grad: float32 [2048, 1024], P('dp', 'tensor')
- w_gate_head_grad: float32 [2048, 16], P('dp', 'tensor')
- w_output_grad: float32 [2048, 2048], P('tensor', 'dp')
- w_gate_grad: float32 [2048, 6144], P('dp', 'tensor')
- w_up_grad: float32 [2048, 6144], P('dp', 'tensor')
- w_down_grad: float32 [6144, 2048], P('tensor', 'dp')
The draws below stay inside these ranges and needn't reach their ends.
All inputs are finite; a program needn't handle non-finite values.
Results may differ from the reference program's by a relative error of at most 0.023.
Values may be sent and summed in bfloat16 or wider, within the bound.
No kernel may reach another device: no remote copies, remote signals or barrier semaphores. Data moves between devices by JAX's collectives and lax.ppermute only.
A program may use at most 320 MiB of HBM per device.

```python
import jax
import jax.numpy as jnp
from jax import lax

MODEL_WIDTH = 2048
QUERY_HEADS = 16
KEY_VALUE_HEADS = 8
HEAD_SIZE = 128
FF = 6144
SEQ_LEN = 1024
SEQS = 16


def touch_ends(entries, own_key, smallest, high):
    index_at = [jax.random.randint(jax.random.fold_in(own_key, axis), (), 0, length) for axis, length in enumerate(entries.shape)]
    widest = entries.shape.index(max(entries.shape))
    neighbour = index_at[:widest] + [(index_at[widest] + 1) % entries.shape[widest]] + index_at[widest + 1:]
    return entries.at[tuple(index_at)].set(smallest).at[tuple(neighbour)].set(high)


def levels(own_key, extent, cuts, smallest, largest):
    level = 1.0
    for dim, parts in cuts:
        heights = jax.random.uniform(jax.random.fold_in(jax.random.fold_in(own_key, 6), dim), (parts,), jnp.float32, smallest / len(cuts), largest / len(cuts))
        level = level * jnp.repeat(jnp.exp(heights), extent[dim] // parts).reshape((-1,) + (1,) * (len(extent) - 1 - dim))
    return level


def centred(stream_key, shape, scale, limit, split=(), kind=jnp.bfloat16):
    values = scale * jax.random.normal(stream_key, shape, jnp.float32)
    if split:
        values = values * levels(stream_key, shape, split, -0.22, 0.18)
    return jnp.clip(values, -limit, limit).astype(kind)


def setup_inputs(seed: int = 0) -> dict:
    seeds = jax.random.split(jax.random.key(seed), 13)
    return {
        "layer_input": centred(seeds[0], (SEQS, SEQ_LEN, MODEL_WIDTH), 1.0, 6.0, ((0, 8), (1, 4))),
        "prefix_lengths": touch_ends(jax.random.randint(seeds[1], (SEQS,), SEQ_LEN // 10, SEQ_LEN // 2 + 1), jax.random.fold_in(seeds[1], 1), SEQ_LEN // 10, (SEQ_LEN // 2 + 1) - 1).astype(jnp.int32),
        "gains": jnp.clip(0.5 + 2.0 * jax.random.uniform(seeds[2], (2 * MODEL_WIDTH + 2 * HEAD_SIZE,), jnp.float32) ** levels(seeds[2], (2 * MODEL_WIDTH + 2 * HEAD_SIZE,), ((0, 32),), -0.2, 0.2), 0.5, 2.5),
        "w_query": centred(seeds[3], (MODEL_WIDTH, QUERY_HEADS * HEAD_SIZE), MODEL_WIDTH ** -0.5, 0.125, ((0, 8), (1, 4))),
        "key_matrix": centred(seeds[4], (MODEL_WIDTH, KEY_VALUE_HEADS * HEAD_SIZE), MODEL_WIDTH ** -0.5, 0.125, ((0, 8), (1, 4))),
        "value_matrix": centred(seeds[5], (MODEL_WIDTH, KEY_VALUE_HEADS * HEAD_SIZE), MODEL_WIDTH ** -0.5, 0.125, ((0, 8), (1, 4))),
        "w_gate_head": centred(seeds[6], (MODEL_WIDTH, QUERY_HEADS), MODEL_WIDTH ** -0.5, 0.125, ((0, 8), (1, 4))),
        "w_output": centred(seeds[7], (QUERY_HEADS * HEAD_SIZE, MODEL_WIDTH), (QUERY_HEADS * HEAD_SIZE // 64) ** -0.5, 1.0, ((0, 4), (1, 8))),
        "w_gate": centred(seeds[8], (MODEL_WIDTH, FF), MODEL_WIDTH ** -0.5, 0.125, ((0, 8), (1, 4))),
        "w_up": centred(seeds[9], (MODEL_WIDTH, FF), MODEL_WIDTH ** -0.5, 0.125, ((0, 8), (1, 4))),
        "w_down": centred(seeds[10], (FF, MODEL_WIDTH), FF ** -0.5, 0.078125, ((0, 4), (1, 8))),
        "out_grad": centred(seeds[11], (SEQS, SEQ_LEN, MODEL_WIDTH), 1.0, 6.0, ((0, 8), (1, 4))),
    }


@jax.custom_vjp
def reduced_precision(v):
    return lax.optimization_barrier(v.astype(jnp.bfloat16)).astype(jnp.float32)

@jax.custom_vjp
def reduced_backward(v):
    return v

def low_keep(v):
    return (reduced_precision(v), None)

def low_pass(kept, grad):
    return (grad,)

def back_keep(v):
    return (v, None)

def back_low(kept, grad):
    return (reduced_precision(grad),)
reduced_precision.defvjp(low_keep, low_pass)
reduced_backward.defvjp(back_keep, back_low)
EPS = 1e-06
THETA = 1000000.0
HIGH = lax.Precision.HIGHEST

def matrix_product(left, right):
    return jnp.dot(left, right, precision=HIGH, preferred_element_type=jnp.float32)

def scaled_norm(value, gain):
    return value * lax.rsqrt(lax.optimization_barrier(jnp.mean(value * value, axis=-1, keepdims=True)) + EPS) * gain

def rope_tables(span_length, width):
    half = width // 2
    freq = THETA ** (-(jnp.arange(half).astype(jnp.float32) * 2.0 / width))
    angle = jnp.arange(span_length).astype(jnp.float32)[:, None] * freq[None, :]
    return (jnp.cos(angle), jnp.sin(angle))

def rotate(value, cosine_table, sine_table):
    half = value.shape[-1] // 2
    first = value[..., :half]
    second = value[..., half:]
    cos_part = cosine_table[:, None, :]
    sin_part = sine_table[:, None, :]
    return jnp.concatenate([first * cos_part - second * sin_part, second * cos_part + first * sin_part], axis=-1)

def prepare_heads(projection, gain, cosine_table, sine_table):
    return rotate(scaled_norm(projection, gain), cosine_table, sine_table)

def attend(query_heads, key_rows, value_rows, prefix):
    span_length = query_heads.shape[0]
    tile_block = min(512, span_length)
    query_group = QUERY_HEADS // KEY_VALUE_HEADS
    columns = jnp.arange(span_length, dtype=jnp.int32)

    def one_block(index):
        start_offset = index * tile_block
        query_token_rows = lax.dynamic_slice_in_dim(query_heads, start_offset, tile_block, 0).reshape(tile_block, KEY_VALUE_HEADS, query_group, HEAD_SIZE)
        scores = jnp.einsum('qkgd,tkd->kgqt', query_token_rows, key_rows, precision=HIGH) * HEAD_SIZE ** (-0.5)
        scores = reduced_backward(scores)
        rows = start_offset + jnp.arange(tile_block, dtype=jnp.int32)
        allowed = (columns[None, :] <= rows[:, None]) | (columns[None, :] < prefix)
        probs = jax.nn.softmax(jnp.where(allowed, scores, -1e+30), axis=-1)
        mixed = jnp.einsum('kgqt,tkd->qkgd', reduced_precision(probs), value_rows, precision=HIGH)
        return mixed.reshape(tile_block, QUERY_HEADS, HEAD_SIZE)
    blocks = lax.map(jax.checkpoint(one_block), jnp.arange(span_length // tile_block, dtype=jnp.int32))
    return blocks.reshape(span_length, QUERY_HEADS, HEAD_SIZE)

def layer_forward(x_value, prefix, gain_all, w_query, key_matrix, value_matrix, w_gate_head, w_output, w_gate, w_up, w_down):
    span_length = x_value.shape[0]
    gain_attn = gain_all[:MODEL_WIDTH]
    gain_ffn = gain_all[MODEL_WIDTH:2 * MODEL_WIDTH]
    gain_query = gain_all[2 * MODEL_WIDTH:2 * MODEL_WIDTH + HEAD_SIZE]
    key_norm_gain = gain_all[2 * MODEL_WIDTH + HEAD_SIZE:]
    normalized_rows = reduced_precision(scaled_norm(x_value, gain_attn))
    cosine_table, sine_table = rope_tables(span_length, HEAD_SIZE)
    query_heads = reduced_precision(prepare_heads(reduced_backward(matrix_product(normalized_rows, w_query)).reshape(span_length, QUERY_HEADS, HEAD_SIZE), gain_query, cosine_table, sine_table))
    key_rows = reduced_precision(prepare_heads(reduced_backward(matrix_product(normalized_rows, key_matrix)).reshape(span_length, KEY_VALUE_HEADS, HEAD_SIZE), key_norm_gain, cosine_table, sine_table))
    value_rows = reduced_precision(reduced_backward(matrix_product(normalized_rows, value_matrix))).reshape(span_length, KEY_VALUE_HEADS, HEAD_SIZE)
    gate_head = jax.nn.sigmoid(reduced_backward(matrix_product(normalized_rows, w_gate_head)))
    mixed = reduced_backward(attend(query_heads, key_rows, value_rows, prefix))
    gated = reduced_precision((mixed * gate_head[:, :, None]).reshape(span_length, QUERY_HEADS * HEAD_SIZE))
    middle = x_value + reduced_backward(matrix_product(gated, w_output))
    normed_ffn = reduced_precision(scaled_norm(middle, gain_ffn))
    gate = reduced_backward(matrix_product(normed_ffn, w_gate))
    up_part = reduced_backward(matrix_product(normed_ffn, w_up))
    hidden = reduced_precision(jax.nn.silu(gate) * up_part)
    return middle + reduced_backward(matrix_product(hidden, w_down))

def reference(layer_input, prefix_lengths, gains, w_query, key_matrix, value_matrix, w_gate_head, w_output, w_gate, w_up, w_down, out_grad):
    weights = (w_query.astype(jnp.float32), key_matrix.astype(jnp.float32), value_matrix.astype(jnp.float32), w_gate_head.astype(jnp.float32), w_output.astype(jnp.float32), w_gate.astype(jnp.float32), w_up.astype(jnp.float32), w_down.astype(jnp.float32))
    gain_all = gains.astype(jnp.float32)

    def step(totals, item):
        x_value, prefix, cotangent = item

        def forward(x_in, gain_in, wq_in, wk_in, wv_in, wg_in, wo_in, wgate_in, wup_in, wdown_in):
            return layer_forward(x_in, prefix, gain_in, wq_in, wk_in, wv_in, wg_in, wo_in, wgate_in, wup_in, wdown_in)
        output, pull = jax.vjp(forward, x_value.astype(jnp.float32), gain_all, weights[0], weights[1], weights[2], weights[3], weights[4], weights[5], weights[6], weights[7])
        grads = pull(cotangent.astype(jnp.float32))
        new_totals = tuple((acc + term for acc, term in zip(totals, grads[1:])))
        return (new_totals, (output.astype(jnp.bfloat16), grads[0]))
    zeros = (jnp.zeros_like(gain_all),) + tuple((jnp.zeros_like(weight) for weight in weights))
    totals, stacked = lax.scan(step, zeros, (layer_input, prefix_lengths, out_grad))
    return (stacked[0], stacked[1], totals[0], totals[1], totals[2], totals[3], totals[4], totals[5], totals[6], totals[7], totals[8])
```

```python
import jax
import jax.numpy as jnp
from jax import lax
from jax.sharding import PartitionSpec as P

HEAD_SIZE = 128
LANES = 128
EPS = 1e-06
THETA = 1000000.0
BF16 = jnp.bfloat16
F32 = jnp.float32


def inverse_rms(value):
    return lax.rsqrt(jnp.mean(value * value, axis=-1, keepdims=True) + EPS)


def scaled_norm(value, gain):
    return value * inverse_rms(value) * gain


def norm_backward(value, gain, grad):
    inverse = inverse_rms(value)
    weighted = grad * gain
    centre = jnp.mean(weighted * value, axis=-1, keepdims=True)
    return (
        inverse * (weighted - value * (inverse * inverse * centre)),
        jnp.sum(grad * value * inverse, axis=0),
    )


def rope_tables(positions):
    half = HEAD_SIZE // 2
    freq = THETA ** (-(jnp.arange(half).astype(F32) * 2.0 / HEAD_SIZE))
    angle = positions.astype(F32)[:, None] * freq[None, :]
    return (jnp.cos(angle), jnp.sin(angle))


def rotate(value, cosine_table, sine_table):
    half = value.shape[-1] // 2
    first = value[..., :half]
    second = value[..., half:]
    cos_part = cosine_table[:, None, :]
    sin_part = sine_table[:, None, :]
    return jnp.concatenate(
        [first * cos_part - second * sin_part, second * cos_part + first * sin_part], axis=-1
    )


def prepare_heads(projection, gain, cosine_table, sine_table):
    return rotate(scaled_norm(projection, gain), cosine_table, sine_table)


def matmul(left, right):
    return jnp.dot(left, right, preferred_element_type=F32)


def left_product(left, right):
    return lax.dot_general(left, right, (((0,), (0,)), ((), ())), preferred_element_type=F32)


def right_product(left, right):
    return lax.dot_general(left, right, (((1,), (1,)), ((), ())), preferred_element_type=F32)


def swap(value, axis, bit):
    size = lax.axis_size(axis)
    return lax.ppermute(value, axis, [(i, i ^ bit) for i in range(size)])


def small_gather(value, axis):
    index = lax.axis_index(axis)
    bit = 1
    while bit < lax.axis_size(axis):
        other = swap(value, axis, bit)
        low = (index & bit) == 0
        value = jnp.concatenate([jnp.where(low, value, other), jnp.where(low, other, value)])
        bit *= 2
    return value


def small_scatter(value, axis):
    index = lax.axis_index(axis)
    bit = lax.axis_size(axis) // 2
    while bit >= 1:
        half = value.shape[0] // 2
        low = (index & bit) == 0
        first, second = value[:half], value[half:]
        other = swap(jnp.where(low, second, first), axis, bit)
        value = jnp.where(low, first, second) + other
        bit //= 2
    return value


def piece_ids():
    size = lax.axis_size("tensor")
    slots = jnp.arange(size, dtype=jnp.int32)
    if size == 4:
        return lax.axis_index("tensor").astype(jnp.int32) ^ slots
    return slots


def gather_pieces(shard):
    size = lax.axis_size("tensor")
    if size != 4:
        whole = lax.all_gather(shard, "tensor", axis=0)
        return [whole[k] for k in range(size)]
    half = shard.shape[0] // 2
    first = swap(shard, "tensor", 1)
    second = swap(shard, "tensor", 2)
    top = swap(second[:half], "tensor", 1)
    bottom = swap(first[half:], "tensor", 2)
    return [shard, first, second, jnp.concatenate([top, bottom])]


def add(left, right):
    return (left.astype(F32) + right.astype(F32)).astype(BF16)


def reduce_pieces(parts):
    size = lax.axis_size("tensor")
    if size != 4:
        return lax.psum_scatter(
            jnp.concatenate(parts), "tensor", scatter_dimension=0, tiled=True
        ).astype(F32)
    own, first, second, far = parts
    half = own.shape[0] // 2
    top = swap(far[:half], "tensor", 1)
    bottom = swap(far[half:], "tensor", 2)
    to_first = jnp.concatenate([first[:half], add(first[half:], bottom)])
    to_second = jnp.concatenate([add(second[:half], top), second[half:]])
    from_first = swap(to_first, "tensor", 1)
    from_second = swap(to_second, "tensor", 2)
    return own.astype(F32) + from_first.astype(F32) + from_second.astype(F32)


def slots_of(value, count):
    rows = value.shape[0] // count
    return [value[k * rows : (k + 1) * rows] for k in range(count)]


def block_scores(query_heads, key_rows, positions, start_offset, tile_block, prefix):
    query_token_rows = lax.dynamic_slice_in_dim(query_heads, start_offset, tile_block, 0)
    scores = jnp.einsum(
        "qkgd,tkd->kgqt", query_token_rows, key_rows, preferred_element_type=F32
    ) * key_rows.shape[-1] ** (-0.5)
    rows = lax.dynamic_slice_in_dim(positions, start_offset, tile_block, 0)
    allowed = (positions[None, :] <= rows[:, None]) | (positions[None, :] < prefix)
    return (scores, allowed, query_token_rows)


def attend_forward(query_heads, key_rows, value_rows, positions, prefix):
    span_length = query_heads.shape[0]
    tile_block = min(512, span_length)
    outs = []
    logs = []
    for index in range(span_length // tile_block):
        scores, allowed, _ = block_scores(
            query_heads, key_rows, positions, index * tile_block, tile_block, prefix
        )
        masked = jnp.where(allowed, scores, -1e30)
        peak = jnp.max(masked, axis=-1, keepdims=True)
        expo = jnp.exp(masked - peak)
        total = jnp.sum(expo, axis=-1, keepdims=True)
        weights = (expo / total).astype(BF16)
        outs.append(
            jnp.einsum("kgqt,tkd->qkgd", weights, value_rows, preferred_element_type=F32)
        )
        logs.append((peak + jnp.log(total))[..., 0])
    return jnp.concatenate(outs), logs


def attend_backward(query_heads, key_rows, value_rows, positions, prefix, logsum, grad_mixed):
    span_length = query_heads.shape[0]
    tile_block = min(512, span_length)
    scale = key_rows.shape[-1] ** (-0.5)
    grad_query, grad_keys, grad_values = [], 0.0, 0.0
    for index in range(span_length // tile_block):
        start_offset = index * tile_block
        scores, allowed, query_token_rows = block_scores(
            query_heads, key_rows, positions, start_offset, tile_block, prefix
        )
        probs = jnp.where(allowed, jnp.exp(scores - logsum[index][..., None]), 0.0)
        rows_grad = lax.dynamic_slice_in_dim(grad_mixed, start_offset, tile_block, 0)
        grad_probs = jnp.einsum(
            "qkgd,tkd->kgqt", rows_grad, value_rows, preferred_element_type=F32
        )
        centre = jnp.sum(probs * grad_probs, axis=-1, keepdims=True)
        grad_scores = (probs * (grad_probs - centre)).astype(BF16)
        grad_query.append(
            jnp.einsum("kgqt,tkd->qkgd", grad_scores, key_rows, preferred_element_type=F32) * scale
        )
        grad_keys = (
            grad_keys
            + jnp.einsum(
                "kgqt,qkgd->tkd", grad_scores, query_token_rows, preferred_element_type=F32
            )
            * scale
        )
        grad_values = grad_values + jnp.einsum(
            "kgqt,qkgd->tkd", probs.astype(BF16), rows_grad, preferred_element_type=F32
        )
    return (jnp.concatenate(grad_query), grad_keys, grad_values)


def swiglu(gate, up_part):
    return jax.nn.silu(gate) * up_part


def on_device(
    layer_input,
    prefix_lengths,
    gains,
    w_query,
    key_matrix,
    value_matrix,
    w_gate_head,
    w_output,
    w_gate,
    w_up,
    w_down,
    out_grad,
):
    sequences = range(layer_input.shape[0])
    size = lax.axis_size("tensor")
    rows = layer_input.shape[1]
    width = layer_input.shape[2]
    span = rows * size
    query_columns = w_query.shape[1]
    key_columns = key_matrix.shape[1]
    heads = query_columns // HEAD_SIZE
    kv_heads = key_columns // HEAD_SIZE
    query_group = heads // kv_heads

    all_gains = small_gather(small_gather(gains, "tensor"), "dp")
    gain_attn = all_gains[:width]
    gain_ffn = all_gains[width : 2 * width]
    gain_query = all_gains[2 * width : 2 * width + HEAD_SIZE]
    key_norm_gain = all_gains[2 * width + HEAD_SIZE :]

    padded_gate = jnp.pad(w_gate_head, ((0, 0), (0, LANES - w_gate_head.shape[1])))
    w_joint = lax.all_gather(
        jnp.concatenate([w_query, key_matrix, value_matrix, padded_gate], axis=1),
        "dp",
        axis=0,
        tiled=True,
    )
    output_w = lax.all_gather(w_output, "dp", axis=1, tiled=True)
    gate_w = lax.all_gather(w_gate, "dp", axis=0, tiled=True)
    up_w = lax.all_gather(w_up, "dp", axis=0, tiled=True)
    down_w = lax.all_gather(w_down, "dp", axis=1, tiled=True)

    ids = piece_ids()
    positions = (ids[:, None] * rows + jnp.arange(rows, dtype=jnp.int32)[None, :]).reshape(-1)
    cosine_table, sine_table = rope_tables(positions)

    x_rows = [layer_input[s].astype(F32) for s in sequences]
    normed = [
        jnp.concatenate(gather_pieces(scaled_norm(x_rows[s], gain_attn).astype(BF16)))
        for s in sequences
    ]
    cotangent = [jnp.concatenate(gather_pieces(out_grad[s])) for s in sequences]

    saved = []
    middle = []
    for s in sequences:
        joint = matmul(normed[s], w_joint)
        query_proj = joint[:, :query_columns].reshape(span, heads, HEAD_SIZE)
        key_proj = joint[:, query_columns : query_columns + key_columns].reshape(
            span, kv_heads, HEAD_SIZE
        )
        value_rows = (
            joint[:, query_columns + key_columns : query_columns + 2 * key_columns]
            .astype(BF16)
            .reshape(span, kv_heads, HEAD_SIZE)
        )
        gate_logit = joint[:, query_columns + 2 * key_columns :][:, :heads]
        query_heads = (
            prepare_heads(query_proj, gain_query, cosine_table, sine_table)
            .astype(BF16)
            .reshape(span, kv_heads, query_group, HEAD_SIZE)
        )
        key_rows = prepare_heads(key_proj, key_norm_gain, cosine_table, sine_table).astype(BF16)
        mixed, logsum = attend_forward(
            query_heads, key_rows, value_rows, positions, prefix_lengths[s]
        )
        mixed = mixed.reshape(span, heads, HEAD_SIZE)
        gate_head = jax.nn.sigmoid(gate_logit)
        gated = (mixed * gate_head[:, :, None]).astype(BF16).reshape(span, query_columns)
        saved.append(
            (query_proj, key_proj, value_rows, query_heads, key_rows, mixed, logsum, gate_head, gated)
        )
        share = matmul(gated, output_w).astype(BF16)
        middle.append(x_rows[s] + reduce_pieces(slots_of(share, size)))

    normed_ffn = [
        jnp.concatenate(gather_pieces(scaled_norm(middle[s], gain_ffn).astype(BF16)))
        for s in sequences
    ]

    blocks, grad_middle, gain_ffn_terms = [], [], []
    ffn_saved = []
    for s in sequences:
        gate = matmul(normed_ffn[s], gate_w)
        up_part = matmul(normed_ffn[s], up_w)
        hidden = swiglu(gate, up_part).astype(BF16)
        grad_hidden = right_product(cotangent[s], down_w)
        grad_gate, grad_up = jax.vjp(swiglu, gate, up_part)[1](grad_hidden)
        grad_gate = grad_gate.astype(BF16)
        grad_up = grad_up.astype(BF16)
        share = (right_product(grad_gate, gate_w) + right_product(grad_up, up_w)).astype(BF16)
        grad_normed_ffn = reduce_pieces(slots_of(share, size))
        term, gain_term = norm_backward(middle[s], gain_ffn, grad_normed_ffn)
        grad_middle.append(term + out_grad[s].astype(F32))
        gain_ffn_terms.append(gain_term)
        ffn_saved.append((hidden, grad_gate, grad_up))
    branch = [
        jnp.concatenate(gather_pieces(grad_middle[s].astype(BF16))) for s in sequences
    ]
    for s in sequences:
        share = matmul(ffn_saved[s][0], down_w).astype(BF16)
        blocks.append((middle[s] + reduce_pieces(slots_of(share, size))).astype(BF16))

    def weight_grad(left, right):
        total = 0.0
        for s in sequences:
            total = total + left_product(left[s], right[s])
        return total.astype(BF16)

    grad_w_down = weight_grad([f[0] for f in ffn_saved], cotangent)
    grad_w_gate = weight_grad(normed_ffn, [f[1] for f in ffn_saved])
    grad_w_up = weight_grad(normed_ffn, [f[2] for f in ffn_saved])
    scatter = lambda value, dim: lax.psum_scatter(
        value, "dp", scatter_dimension=dim, tiled=True
    ).astype(F32)
    out_down = scatter(grad_w_down, 1)
    out_gate = scatter(grad_w_gate, 0)
    out_up = scatter(grad_w_up, 0)

    grad_w_output = weight_grad([a[8] for a in saved], branch)
    out_output = scatter(grad_w_output, 1)
    joint_grads, input_rows, gain_attn_terms, head_gain_terms = [], [], [], []
    for s in sequences:
        query_proj, key_proj, value_rows, query_heads, key_rows, mixed, logsum, gate_head, _ = saved[s]
        grad_gated = right_product(branch[s], output_w).reshape(span, heads, HEAD_SIZE)
        grad_mixed = (grad_gated * gate_head[:, :, None]).astype(BF16)
        grad_gate_logit = (
            jnp.sum(grad_gated * mixed, axis=-1) * gate_head * (1.0 - gate_head)
        ).astype(BF16)
        grad_query, grad_keys, grad_values = attend_backward(
            query_heads,
            key_rows,
            value_rows,
            positions,
            prefix_lengths[s],
            logsum,
            grad_mixed.reshape(span, kv_heads, query_group, HEAD_SIZE),
        )
        prepare = lambda proj, gain: prepare_heads(proj, gain, cosine_table, sine_table)
        grad_query_proj, grad_gain_query = jax.vjp(prepare, query_proj, gain_query)[1](
            grad_query.reshape(span, heads, HEAD_SIZE)
        )
        grad_key_proj, grad_gain_key = jax.vjp(prepare, key_proj, key_norm_gain)[1](grad_keys)
        joint_grad = jnp.concatenate(
            [
                grad_query_proj.astype(BF16).reshape(span, query_columns),
                grad_key_proj.astype(BF16).reshape(span, key_columns),
                grad_values.astype(BF16).reshape(span, key_columns),
                jnp.pad(grad_gate_logit, ((0, 0), (0, LANES - heads))),
            ],
            axis=1,
        )
        joint_grads.append(joint_grad)
        share = right_product(joint_grad, w_joint).astype(BF16)
        grad_rows, gain_term = norm_backward(
            x_rows[s], gain_attn, reduce_pieces(slots_of(share, size))
        )
        input_rows.append(grad_middle[s] + grad_rows)
        gain_attn_terms.append(gain_term)
        head_gain_terms.append(jnp.concatenate([grad_gain_query, grad_gain_key]))
    out_joint = scatter(weight_grad(normed, joint_grads), 0)
    total = lambda terms: sum(terms[1:], terms[0])
    gain_total = jnp.concatenate(
        [total(gain_attn_terms), total(gain_ffn_terms), total(head_gain_terms)]
    )
    gains_grad = small_scatter(small_scatter(gain_total, "dp"), "tensor")
    value_start = query_columns + key_columns
    gate_start = value_start + key_columns
    return (
        jnp.stack(blocks),
        jnp.stack(input_rows),
        gains_grad,
        out_joint[:, :query_columns],
        out_joint[:, query_columns:value_start],
        out_joint[:, value_start:gate_start],
        out_joint[:, gate_start : gate_start + heads],
        out_output,
        out_gate,
        out_up,
        out_down,
    )


def solution(mesh):
    placed = (
        P("dp", "tensor", None),
        P("dp"),
        P(("dp", "tensor")),
        P("dp", "tensor"),
        P("dp", "tensor"),
        P("dp", "tensor"),
        P("dp", "tensor"),
        P("tensor", "dp"),
        P("dp", "tensor"),
        P("dp", "tensor"),
        P("tensor", "dp"),
        P("dp", "tensor", None),
    )
    return jax.shard_map(
        on_device,
        mesh=mesh,
        in_specs=placed,
        out_specs=(
            P("dp", "tensor", None),
            P("dp", "tensor", None),
            P(("dp", "tensor")),
            P("dp", "tensor"),
            P("dp", "tensor"),
            P("dp", "tensor"),
            P("dp", "tensor"),
            P("tensor", "dp"),
            P("dp", "tensor"),
            P("dp", "tensor"),
            P("tensor", "dp"),
        ),
        check_vma=False,
    )
```

```python
import functools
import math

import jax
import jax.numpy as jnp
from jax import lax
from jax.experimental import pallas as pl
from jax.experimental.pallas import tpu as pltpu
from jax.sharding import PartitionSpec as P


HEAD_SIZE = 128
DP, TENSOR = "dp", "tensor"
LANES = 128
EPS = 1e-06
THETA = 1000000.0
BF16 = jnp.bfloat16
F32 = jnp.float32


def inverse_rms(value):
    return lax.rsqrt(jnp.mean(value * value, axis=-1, keepdims=True) + EPS)


def scaled_norm(value, gain):
    return value * inverse_rms(value) * gain


def norm_backward(value, inverse, gain, grad):
    weighted = grad * gain
    centre = jnp.mean(weighted * value, axis=-1, keepdims=True)
    return (
        inverse * (weighted - value * (inverse * inverse * centre)),
        jnp.sum(grad * value * inverse, axis=0),
    )


def rope_tables(positions):
    half = HEAD_SIZE // 2
    freq = THETA ** (-(jnp.arange(half).astype(F32) * 2.0 / HEAD_SIZE))
    angle = positions.astype(F32)[:, None] * freq[None, :]
    cosine, sine = jnp.cos(angle), jnp.sin(angle)
    return (
        jnp.concatenate([cosine, cosine], axis=1),
        jnp.concatenate([-sine, sine], axis=1),
    )


def matmul(left, right):
    return jnp.dot(left, right, preferred_element_type=F32)


def left_product(left, right):
    return lax.dot_general(left, right, (((0,), (0,)), ((), ())), preferred_element_type=F32)


def right_product(left, right):
    return lax.dot_general(left, right, (((1,), (1,)), ((), ())), preferred_element_type=F32)


def swap(value, axis, bit):
    size = lax.axis_size(axis)
    return lax.ppermute(value, axis, [(i, i ^ bit) for i in range(size)])


def small_gather(value, axis):
    index = lax.axis_index(axis)
    bit = 1
    while bit < lax.axis_size(axis):
        other = swap(value, axis, bit)
        low = (index & bit) == 0
        value = jnp.concatenate([jnp.where(low, value, other), jnp.where(low, other, value)])
        bit *= 2
    return value


def small_scatter(value, axis):
    index = lax.axis_index(axis)
    bit = lax.axis_size(axis) // 2
    while bit >= 1:
        half = value.shape[0] // 2
        low = (index & bit) == 0
        first, second = value[:half], value[half:]
        other = swap(jnp.where(low, second, first), axis, bit)
        value = jnp.where(low, first, second) + other
        bit //= 2
    return value


def piece_ids():
    size = lax.axis_size(TENSOR)
    slots = jnp.arange(size, dtype=jnp.int32)
    if size == 4:
        return lax.axis_index(TENSOR).astype(jnp.int32) ^ slots
    return slots


def gather_start(shard):
    if lax.axis_size(TENSOR) != 4:
        return (lax.all_gather(shard, TENSOR, axis=0, tiled=True),)
    return (shard, swap(shard, TENSOR, 1), swap(shard, TENSOR, 2))


def gather_finish(hop):
    if lax.axis_size(TENSOR) != 4:
        return hop[0]
    shard, first, second = hop
    half = shard.shape[0] // 2
    top = swap(second[:half], TENSOR, 1)
    bottom = swap(first[half:], TENSOR, 2)
    return jnp.concatenate([shard, first, second, top, bottom])


def add(left, right):
    return (left.astype(F32) + right.astype(F32)).astype(BF16)


def reduce_start(share):
    if lax.axis_size(TENSOR) != 4:
        return (share,)
    rows = share.shape[0] // 4
    own, first, second, far = [share[k * rows : (k + 1) * rows] for k in range(4)]
    half = rows // 2
    return (own, first, second, swap(far[:half], TENSOR, 1), swap(far[half:], TENSOR, 2))


def reduce_middle(hop):
    if lax.axis_size(TENSOR) != 4:
        return hop
    own, first, second, top, bottom = hop
    half = top.shape[0]
    return (
        own,
        jnp.concatenate([first[:half], add(first[half:], bottom)]),
        jnp.concatenate([add(second[:half], top), second[half:]]),
    )


def reduce_finish(hop):
    if lax.axis_size(TENSOR) != 4:
        return lax.psum_scatter(hop[0], TENSOR, scatter_dimension=0, tiled=True).astype(F32)
    own, to_first, to_second = hop
    from_first = swap(to_first, TENSOR, 1)
    from_second = swap(to_second, TENSOR, 2)
    return own.astype(F32) + from_first.astype(F32) + from_second.astype(F32)


def rope(value, cosine, sine):
    return value * cosine + pltpu.roll(value, HEAD_SIZE // 2, 1) * sine


def unrope(value, cosine, sine):
    return value * cosine - pltpu.roll(value, HEAD_SIZE // 2, 1) * sine


def dot(left, right, left_dim, right_dim):
    return lax.dot_general(
        left, right, (((left_dim,), (right_dim,)), ((), ())), preferred_element_type=F32
    )


def lane_column(block, lane):
    lanes = lax.broadcasted_iota(jnp.int32, block.shape, 1)
    return jnp.sum(jnp.where(lanes == lane, block, 0.0), axis=-1, keepdims=True)


def tile_visibility(ids_ref, prefix, query_slot, key_slot, rows):
    query_piece = ids_ref[query_slot]
    key_piece = ids_ref[key_slot]
    full = jnp.logical_or(key_piece < query_piece, (key_piece + 1) * rows <= prefix)
    some = jnp.logical_or(key_piece == query_piece, key_piece * rows < prefix)
    return full, jnp.logical_and(some, jnp.logical_not(full)), query_piece * rows, key_piece * rows


def allowed_tile(shape, rows, query_start, key_start, prefix):
    query = lax.rem(lax.broadcasted_iota(jnp.int32, shape, 0), rows) + query_start
    key = lax.broadcasted_iota(jnp.int32, shape, 1) + key_start
    return jnp.logical_or(key <= query, key < prefix)


SCORE_SCALE = HEAD_SIZE ** (-0.5)
LOG2_SCALE = SCORE_SCALE * math.log2(math.e)


def forward_body(
    ids_ref, prefix_ref, q_ref, k_ref, v_ref, gate_ref, cos_q, sin_q, cos_k, sin_k, gain_q, gain_k,
    gated_ref, mixed_ref, log_ref, key_scr, value_scr, sum_scr,
):
    kv_head, slot = pl.program_id(0), pl.program_id(1)
    rows = q_ref.shape[0]
    slots = k_ref.shape[0] // rows
    group = q_ref.shape[1] // HEAD_SIZE
    prefix = prefix_ref[0]

    @pl.when(slot == 0)
    def _():
        key_scr[...] = rope(scaled_norm(k_ref[...], gain_k[...]), cos_k[...], sin_k[...]).astype(BF16)
        value_scr[:, :HEAD_SIZE] = v_ref[...].astype(BF16)
        value_scr[:, HEAD_SIZE:] = jnp.ones_like(value_scr[:, HEAD_SIZE:])

    query = jnp.concatenate(
        [
            rope(
                scaled_norm(q_ref[:, h * HEAD_SIZE : (h + 1) * HEAD_SIZE], gain_q[...]),
                cos_q[...],
                sin_q[...],
            ).astype(BF16)
            for h in range(group)
        ]
    )
    sum_scr[...] = jnp.zeros_like(sum_scr)

    for key_slot in range(slots):
        full, partial, query_start, key_start = tile_visibility(
            ids_ref, prefix, slot, key_slot, rows
        )
        tile = slice(key_slot * rows, (key_slot + 1) * rows)

        def step(masked):
            expo = jnp.exp2(dot(query, key_scr[tile, :], 1, 1) * LOG2_SCALE)
            if masked:
                expo = jnp.where(
                    allowed_tile(expo.shape, rows, query_start, key_start, prefix), expo, 0.0
                )
            sum_scr[...] += dot(expo.astype(BF16), value_scr[tile, :], 1, 0)

        pl.when(full)(functools.partial(step, False))
        pl.when(partial)(functools.partial(step, True))

    gate = jax.nn.sigmoid(gate_ref[...])
    for h in range(group):
        part = slice(h * rows, (h + 1) * rows)
        columns = slice(h * HEAD_SIZE, (h + 1) * HEAD_SIZE)
        total = sum_scr[part, HEAD_SIZE:]
        mixed = sum_scr[part, :HEAD_SIZE] / total
        mixed_ref[:, columns] = mixed
        log_ref[:, columns] = jnp.log2(total)
        gated_ref[:, columns] = (mixed * lane_column(gate, kv_head * group + h)).astype(BF16)


def head_norm_backward(value, gain, grad):
    inverse = inverse_rms(value)
    weighted = grad * gain
    centre = jnp.mean(weighted * value, axis=-1, keepdims=True)
    return (
        inverse * (weighted - value * (inverse * inverse * centre)),
        jnp.sum(grad * value * inverse, axis=0, keepdims=True),
    )


def backward_body(
    ids_ref, prefix_ref, q_ref, k_ref, v_ref, gate_ref, cos_q, sin_q, cos_k, sin_k, gain_q, gain_k,
    grad_ref, mixed_ref, log_ref,
    joint_ref, gains_ref, key_scr, value_scr, grad_key_scr, grad_value_scr, grad_query_scr, gate_scr,
    gain_scr,
):
    kv_head, slot = pl.program_id(0), pl.program_id(1)
    rows = q_ref.shape[0]
    slots = k_ref.shape[0] // rows
    group = q_ref.shape[1] // HEAD_SIZE
    kv_heads = pl.num_programs(0)
    prefix = prefix_ref[0]

    @pl.when(jnp.logical_and(slot == 0, kv_head == 0))
    def _():
        gate_scr[...] = jnp.zeros_like(gate_scr)
        gain_scr[...] = jnp.zeros_like(gain_scr)

    @pl.when(slot == 0)
    def _():
        key_scr[...] = rope(scaled_norm(k_ref[...], gain_k[...]), cos_k[...], sin_k[...]).astype(BF16)
        value_scr[...] = v_ref[...].astype(BF16)
        grad_key_scr[...] = jnp.zeros_like(grad_key_scr)
        grad_value_scr[...] = jnp.zeros_like(grad_value_scr)

    row_start = pl.multiple_of(slot * rows, rows)
    gate = jax.nn.sigmoid(gate_ref[...])
    lanes = lax.broadcasted_iota(jnp.int32, gate.shape, 1)
    query, mixed_grad, centre = [], [], []
    gate_grad = jnp.zeros_like(gate)
    for h in range(group):
        columns = slice(h * HEAD_SIZE, (h + 1) * HEAD_SIZE)
        query.append(
            rope(scaled_norm(q_ref[:, columns], gain_q[...]), cos_q[...], sin_q[...]).astype(BF16)
        )
        head_gate = lane_column(gate, kv_head * group + h)
        grad = grad_ref[:, columns]
        product = jnp.sum(grad * mixed_ref[:, columns], axis=-1, keepdims=True)
        gate_grad = gate_grad + jnp.where(
            lanes == kv_head * group + h, product * head_gate * (1.0 - head_gate), 0.0
        )
        low = (grad * head_gate).astype(BF16)
        mixed_grad.append(low)
        centre.append(
            jnp.sum(low.astype(F32) * mixed_ref[:, columns], axis=-1, keepdims=True)
        )
    gate_scr[pl.ds(row_start, rows), :] += gate_grad
    query = jnp.concatenate(query)
    mixed_grad = jnp.concatenate(mixed_grad)
    centre = jnp.concatenate(centre)
    logs = jnp.concatenate(
        [log_ref[:, h * HEAD_SIZE : h * HEAD_SIZE + 1] for h in range(group)]
    )
    grad_query_scr[...] = jnp.zeros_like(grad_query_scr)

    for key_slot in range(slots):
        full, partial, query_start, key_start = tile_visibility(
            ids_ref, prefix, slot, key_slot, rows
        )
        tile = slice(key_slot * rows, (key_slot + 1) * rows)

        def step(masked):
            probs = jnp.exp2(dot(query, key_scr[tile, :], 1, 1) * LOG2_SCALE - logs)
            if masked:
                probs = jnp.where(
                    allowed_tile(probs.shape, rows, query_start, key_start, prefix), probs, 0.0
                )
            grad_probs = dot(mixed_grad, value_scr[tile, :], 1, 1)
            grad_scores = (probs * (grad_probs - centre)).astype(BF16)
            grad_query_scr[...] += dot(grad_scores, key_scr[tile, :], 1, 0)
            grad_key_scr[tile, :] += dot(grad_scores, query, 0, 0)
            grad_value_scr[tile, :] += dot(probs.astype(BF16), mixed_grad, 0, 0)

        pl.when(full)(functools.partial(step, False))
        pl.when(partial)(functools.partial(step, True))

    for h in range(group):
        columns = slice(h * HEAD_SIZE, (h + 1) * HEAD_SIZE)
        grad = unrope(
            grad_query_scr[h * rows : (h + 1) * rows, :] * SCORE_SCALE, cos_q[...], sin_q[...]
        )
        value, term = head_norm_backward(q_ref[:, columns], gain_q[...], grad)
        gain_scr[0:1, :] += term
        start = pl.multiple_of((kv_head * group + h) * HEAD_SIZE, HEAD_SIZE)
        joint_ref[pl.ds(row_start, rows), pl.ds(start, HEAD_SIZE)] = value.astype(BF16)

    @pl.when(slot == slots - 1)
    def _():
        grad = unrope(grad_key_scr[...] * SCORE_SCALE, cos_k[...], sin_k[...])
        value, term = head_norm_backward(k_ref[...], gain_k[...], grad)
        gain_scr[1:2, :] += term
        start = pl.multiple_of((kv_heads * group + kv_head) * HEAD_SIZE, HEAD_SIZE)
        joint_ref[:, pl.ds(start, HEAD_SIZE)] = value.astype(BF16)
        start = pl.multiple_of((kv_heads * (group + 1) + kv_head) * HEAD_SIZE, HEAD_SIZE)
        joint_ref[:, pl.ds(start, HEAD_SIZE)] = grad_value_scr[...].astype(BF16)

    @pl.when(jnp.logical_and(slot == slots - 1, kv_head == kv_heads - 1))
    def _():
        joint_ref[:, joint_ref.shape[1] - LANES :] = gate_scr[...].astype(BF16)
        gains_ref[...] = gain_scr[...]


def attention_specs(span, slots, heads, kv_heads):
    rows = span // slots
    group = heads // kv_heads
    whole = lambda column: pl.BlockSpec((span, HEAD_SIZE), lambda g, i, *_: (0, column(g)))
    return [
        pl.BlockSpec((rows, group * HEAD_SIZE), lambda g, i, *_: (i, g)),
        whole(lambda g: heads + g),
        whole(lambda g: heads + kv_heads + g),
        pl.BlockSpec((rows, LANES), lambda g, i, *_: (i, heads + 2 * kv_heads)),
        pl.BlockSpec((rows, HEAD_SIZE), lambda g, i, *_: (i, 0)),
        pl.BlockSpec((rows, HEAD_SIZE), lambda g, i, *_: (i, 0)),
        whole(lambda g: 0),
        whole(lambda g: 0),
        pl.BlockSpec((1, HEAD_SIZE), lambda g, i, *_: (0, 0)),
        pl.BlockSpec((1, HEAD_SIZE), lambda g, i, *_: (0, 0)),
    ]


def attention_forward(ids, prefix, joint, cosine, sine, gain_q, gain_k, heads, kv_heads):
    span, slots = joint.shape[0], ids.shape[0]
    rows, group = span // slots, heads // kv_heads
    block = pl.BlockSpec((rows, group * HEAD_SIZE), lambda g, i, *_: (i, g))
    return pl.pallas_call(
        forward_body,
        grid_spec=pltpu.PrefetchScalarGridSpec(
            num_scalar_prefetch=2,
            grid=(kv_heads, slots),
            in_specs=attention_specs(span, slots, heads, kv_heads),
            out_specs=[block, block, block],
            scratch_shapes=[
                pltpu.VMEM((span, HEAD_SIZE), BF16),
                pltpu.VMEM((span, 2 * HEAD_SIZE), BF16),
                pltpu.VMEM((group * rows, 2 * HEAD_SIZE), F32),
            ],
        ),
        out_shape=[
            jax.ShapeDtypeStruct((span, heads * HEAD_SIZE), BF16),
            jax.ShapeDtypeStruct((span, heads * HEAD_SIZE), F32),
            jax.ShapeDtypeStruct((span, heads * HEAD_SIZE), F32),
        ],
        cost_estimate=pl.CostEstimate(
            flops=3 * heads * span * span * HEAD_SIZE,
            bytes_accessed=joint.size * 4 + span * heads * HEAD_SIZE * 10,
            transcendentals=heads * span * span,
        ),
        name="attention_forward",
    )(ids, prefix, joint, joint, joint, joint, cosine, sine, cosine, sine, gain_q, gain_k)


def attention_backward(
    ids, prefix, joint, cosine, sine, gain_q, gain_k, grad, mixed, logs, heads, kv_heads
):
    span, slots = joint.shape[0], ids.shape[0]
    rows, group = span // slots, heads // kv_heads
    block = pl.BlockSpec((rows, group * HEAD_SIZE), lambda g, i, *_: (i, g))
    return pl.pallas_call(
        backward_body,
        grid_spec=pltpu.PrefetchScalarGridSpec(
            num_scalar_prefetch=2,
            grid=(kv_heads, slots),
            in_specs=attention_specs(span, slots, heads, kv_heads) + [block, block, block],
            out_specs=[
                pl.BlockSpec(joint.shape, lambda g, i, *_: (0, 0)),
                pl.BlockSpec((8, HEAD_SIZE), lambda g, i, *_: (0, 0)),
            ],
            scratch_shapes=[
                pltpu.VMEM((span, HEAD_SIZE), BF16),
                pltpu.VMEM((span, HEAD_SIZE), BF16),
                pltpu.VMEM((span, HEAD_SIZE), F32),
                pltpu.VMEM((span, HEAD_SIZE), F32),
                pltpu.VMEM((group * rows, HEAD_SIZE), F32),
                pltpu.VMEM((span, LANES), F32),
                pltpu.VMEM((8, HEAD_SIZE), F32),
            ],
        ),
        out_shape=[
            jax.ShapeDtypeStruct(joint.shape, BF16),
            jax.ShapeDtypeStruct((8, HEAD_SIZE), F32),
        ],
        cost_estimate=pl.CostEstimate(
            flops=8 * heads * span * span * HEAD_SIZE,
            bytes_accessed=joint.size * 6 + span * heads * HEAD_SIZE * 12,
            transcendentals=heads * span * span,
        ),
        name="attention_backward",
    )(
        ids, prefix, joint, joint, joint, joint, cosine, sine, cosine, sine, gain_q, gain_k,
        grad, mixed, logs,
    )


def middle_body(joint_ref, cotangent_ref, down_ref, hidden_ref, grad_ref):
    width = hidden_ref.shape[1]
    chunk = min(256, hidden_ref.shape[0])
    for start in range(0, hidden_ref.shape[0], chunk):
        rows = slice(start, start + chunk)
        grad = dot(cotangent_ref[rows, :], down_ref[...], 1, 1)
        gate = joint_ref[rows, :width]
        up = joint_ref[rows, width:]
        sigmoid = jax.nn.sigmoid(gate)
        silu = gate * sigmoid
        hidden_ref[rows, :] = (silu * up).astype(BF16)
        grad_ref[rows, :width] = (grad * up * (sigmoid * (1.0 + gate * (1.0 - sigmoid)))).astype(BF16)
        grad_ref[rows, width:] = (grad * silu).astype(BF16)


def feedforward_middle(joint, cotangent, down, block):
    span, hidden, width = joint.shape[0], down.shape[0], down.shape[1]
    return pl.pallas_call(
        middle_body,
        grid=(hidden // block,),
        in_specs=[
            pl.BlockSpec((span, 2 * block), lambda h: (0, h)),
            pl.BlockSpec((span, width), lambda h: (0, 0)),
            pl.BlockSpec((block, width), lambda h: (h, 0)),
        ],
        out_specs=[
            pl.BlockSpec((span, block), lambda h: (0, h)),
            pl.BlockSpec((span, 2 * block), lambda h: (0, h)),
        ],
        out_shape=[
            jax.ShapeDtypeStruct((span, hidden), BF16),
            jax.ShapeDtypeStruct((span, 2 * hidden), BF16),
        ],
        cost_estimate=pl.CostEstimate(
            flops=2 * span * hidden * width,
            bytes_accessed=joint.size * 6 + cotangent.size * 2 + down.size * 2,
            transcendentals=span * hidden,
        ),
        name="feedforward_middle",
    )(joint, cotangent, down)


def interleave(left, right, block):
    parts = []
    for start in range(0, left.shape[1], block):
        parts += [left[:, start : start + block], right[:, start : start + block]]
    return jnp.concatenate(parts, axis=1)


def separate(value, block):
    take = lambda first: jnp.concatenate(
        [value[:, k : k + block] for k in range(first, value.shape[1], 2 * block)], axis=1
    )
    return take(0), take(block)


def on_device(
    layer_input,
    prefix_lengths,
    gains,
    w_query,
    key_matrix,
    value_matrix,
    w_gate_head,
    w_output,
    w_gate,
    w_up,
    w_down,
    out_grad,
):
    sequences = range(layer_input.shape[0])
    rows = layer_input.shape[1]
    width = layer_input.shape[2]
    query_columns = w_query.shape[1]
    key_columns = key_matrix.shape[1]
    heads = query_columns // HEAD_SIZE
    kv_heads = key_columns // HEAD_SIZE

    all_gains = small_gather(small_gather(gains, TENSOR), DP)
    gain_attn = all_gains[:width]
    gain_ffn = all_gains[width : 2 * width]
    gain_query = all_gains[2 * width : 2 * width + HEAD_SIZE].reshape(1, -1)
    key_norm_gain = all_gains[2 * width + HEAD_SIZE :].reshape(1, -1)

    padded_gate = jnp.pad(w_gate_head, ((0, 0), (0, LANES - w_gate_head.shape[1])))
    block = math.gcd(256, w_gate.shape[1])
    w_joint = lax.all_gather(
        jnp.concatenate([w_query, key_matrix, value_matrix, padded_gate], axis=1),
        DP,
        axis=0,
        tiled=True,
    )
    output_w = lax.all_gather(w_output, DP, axis=1, tiled=True)
    both_w = lax.all_gather(interleave(w_gate, w_up, block), DP, axis=0, tiled=True)
    down_w = lax.all_gather(w_down, DP, axis=1, tiled=True)

    ids = piece_ids()
    positions = (ids[:, None] * rows + jnp.arange(rows, dtype=jnp.int32)[None, :]).reshape(-1)
    cosine_table, sine_table = rope_tables(positions)
    barrier = lax.optimization_barrier

    def scatter(value, dim):
        shard = lax.psum_scatter(value, DP, scatter_dimension=dim, tiled=True)
        return shard.astype(F32)


    late = lambda value, after: barrier((value, after))[0]
    inputs = [barrier(layer_input[s]) for s in sequences]
    grads = [barrier(out_grad[s]) for s in sequences]
    x_rows = [inputs[s].astype(F32) for s in sequences]
    inverses = [barrier(inverse_rms(x_rows[s])) for s in sequences]
    low = [barrier((x_rows[s] * inverses[s] * gain_attn).astype(BF16)) for s in sequences]
    cotangent = [gather_finish(gather_start(grads[s])) for s in sequences]
    normed = [gather_finish(gather_start(low[s])) for s in sequences]

    joints, gated, mixed, logs, middle, ffn_low, normed_ffn = [], [], [], [], [], [], []
    hops, ffn_inverses = [], []
    for s in sequences:
        joints.append(matmul(normed[s], w_joint))
        outs = attention_forward(
            ids, prefix_lengths[s : s + 1], joints[s], cosine_table, sine_table, gain_query,
            key_norm_gain, heads, kv_heads,
        )
        for kept, out in zip((gated, mixed, logs), outs):
            kept.append(out)
        share = matmul(gated[s], output_w).astype(BF16)
        hops.append(reduce_middle(reduce_start(share)))
    opened = ()
    for s in sequences:
        hop = hops[s] if s == 0 else barrier((hops[s], ffn_low[s - 1]))[0]
        x_late, gain_late = late((inputs[s], gain_ffn), (hop, opened))
        middle.append(barrier(x_late.astype(F32) + reduce_finish(hop)))
        ffn_inverses.append(barrier(inverse_rms(middle[s])))
        ffn_low.append(barrier((middle[s] * ffn_inverses[s] * gain_late).astype(BF16)))
        opened = gather_start(ffn_low[s])
        normed_ffn.append(gather_finish(opened))

    hidden, grad_both, grad_middle, gain_ffn_terms, branch = [], [], [], [], []
    hops = []
    for s in sequences:
        gate_up = matmul(normed_ffn[s], both_w)
        outs = feedforward_middle(gate_up, cotangent[s], down_w, block)
        hidden.append(outs[0])
        grad_both.append(outs[1])
        share = right_product(grad_both[s], both_w).astype(BF16)
        hops.append(reduce_middle(reduce_start(share)))
    for s in sequences:
        hop = hops[s] if s == 0 else barrier((hops[s], grad_middle[s - 1]))[0]
        middle_late, inverse_late, grad_late, gain_late = late(
            (middle[s], ffn_inverses[s], grads[s], gain_ffn), hop
        )
        term, gain_term = norm_backward(middle_late, inverse_late, gain_late, reduce_finish(hop))
        gain_ffn_terms.append(barrier(gain_term))
        grad_middle.append(barrier(term + grad_late.astype(F32)))
        branch.append(gather_finish(gather_start(grad_middle[s].astype(BF16))))

    def weight_grad(left, right):
        total = left_product(left[0], right[0])
        for s in sequences[1:]:
            total = left_product(left[s], right[s]) + total
        return total.astype(BF16)

    out_down = scatter(weight_grad(hidden, cotangent), 1)
    out_both = scatter(weight_grad(normed_ffn, grad_both), 0)

    joint_grads, head_gain_terms, blocks, input_rows, gain_attn_terms = [], [], [], [], []
    hops = []
    for s in sequences:
        share = matmul(hidden[s], down_w).astype(BF16)
        hop = reduce_middle(reduce_start(share))
        middle_late = late(middle[s], hop)
        blocks.append(barrier((middle_late + reduce_finish(hop)).astype(BF16)))
        grad_gated = right_product(branch[s], output_w)
        joint_grad, head_gains = attention_backward(
            ids, prefix_lengths[s : s + 1], joints[s], cosine_table, sine_table, gain_query,
            key_norm_gain, grad_gated, mixed[s], logs[s], heads, kv_heads,
        )
        joint_grads.append(joint_grad)
        head_gain_terms.append(head_gains[:2].reshape(-1))
        share = right_product(joint_grads[s], w_joint).astype(BF16)
        hops.append(reduce_middle(reduce_start(share)))
    for s in sequences:
        hop = hops[s] if s == 0 else barrier((hops[s], input_rows[s - 1]))[0]
        x_late, inverse_late, grad_late, gain_late = late(
            (inputs[s], inverses[s], grad_middle[s], gain_attn), hop
        )
        grad_rows, gain_term = norm_backward(
            x_late.astype(F32), inverse_late, gain_late, reduce_finish(hop)
        )
        gain_attn_terms.append(barrier(gain_term))
        input_rows.append(barrier(grad_late + grad_rows))
    out_output = scatter(weight_grad(gated, branch), 1)
    out_joint = scatter(weight_grad(normed, joint_grads), 0)
    out_gate, out_up = separate(out_both, block)
    total = lambda terms: sum(terms[1:], terms[0])
    gain_total = jnp.concatenate(
        [total(gain_attn_terms), total(gain_ffn_terms), total(head_gain_terms)]
    )
    gains_grad = small_scatter(small_scatter(gain_total, DP), TENSOR)
    value_start = query_columns + key_columns
    gate_start = value_start + key_columns
    return (
        jnp.stack(blocks),
        jnp.stack(input_rows),
        gains_grad,
        out_joint[:, :query_columns],
        out_joint[:, query_columns:value_start],
        out_joint[:, value_start:gate_start],
        out_joint[:, gate_start : gate_start + heads],
        out_output,
        out_gate,
        out_up,
        out_down,
    )


def solution(mesh):
    rows = P(DP, TENSOR, None)
    gain = P((DP, TENSOR))
    into, out_of = P(DP, TENSOR), P(TENSOR, DP)
    weights = (into, into, into, into, out_of, into, into, out_of)

    return jax.shard_map(
        on_device,
        mesh=mesh,
        in_specs=(rows, P(DP), gain) + weights + (rows,),
        out_specs=(rows, rows, gain) + weights,
        check_vma=False,
    )
```

```python
import functools
import math

import jax
import jax.numpy as jnp
from jax import lax
from jax.experimental import pallas as pl
from jax.experimental.pallas import tpu as pltpu
from jax.sharding import PartitionSpec as P


HEAD_SIZE = 128
DP, TENSOR = "dp", "tensor"
LANES = 128
EPS = 1e-06
THETA = 1000000.0
BF16 = jnp.bfloat16
F32 = jnp.float32


def inverse_rms(value):
    return lax.rsqrt(jnp.mean(value * value, axis=-1, keepdims=True) + EPS)


def scaled_norm(value, gain):
    return value * inverse_rms(value) * gain


def norm_backward(value, inverse, gain, grad):
    weighted = grad * gain
    centre = jnp.mean(weighted * value, axis=-1, keepdims=True)
    return (
        inverse * (weighted - value * (inverse * inverse * centre)),
        jnp.sum(grad * value * inverse, axis=0),
    )


def rope_tables(positions):
    half = HEAD_SIZE // 2
    freq = THETA ** (-(jnp.arange(half).astype(F32) * 2.0 / HEAD_SIZE))
    angle = positions.astype(F32)[:, None] * freq[None, :]
    cosine, sine = jnp.cos(angle), jnp.sin(angle)
    return (
        jnp.concatenate([cosine, cosine], axis=1),
        jnp.concatenate([-sine, sine], axis=1),
    )


def matmul(left, right):
    return jnp.dot(left, right, preferred_element_type=F32)


def left_product(left, right):
    return lax.dot_general(left, right, (((0,), (0,)), ((), ())), preferred_element_type=F32)


def right_product(left, right):
    return lax.dot_general(left, right, (((1,), (1,)), ((), ())), preferred_element_type=F32)


def swap(value, axis, bit):
    size = lax.axis_size(axis)
    return lax.ppermute(value, axis, [(i, i ^ bit) for i in range(size)])


def small_gather(value, axis):
    index = lax.axis_index(axis)
    bit = 1
    while bit < lax.axis_size(axis):
        other = swap(value, axis, bit)
        low = (index & bit) == 0
        value = jnp.concatenate([jnp.where(low, value, other), jnp.where(low, other, value)])
        bit *= 2
    return value


def small_scatter(value, axis):
    index = lax.axis_index(axis)
    bit = lax.axis_size(axis) // 2
    while bit >= 1:
        half = value.shape[0] // 2
        low = (index & bit) == 0
        first, second = value[:half], value[half:]
        other = swap(jnp.where(low, second, first), axis, bit)
        value = jnp.where(low, first, second) + other
        bit //= 2
    return value


def piece_ids():
    size = lax.axis_size(TENSOR)
    slots = jnp.arange(size, dtype=jnp.int32)
    if size == 4:
        return lax.axis_index(TENSOR).astype(jnp.int32) ^ slots
    return slots


def gather_start(shard):
    if lax.axis_size(TENSOR) != 4:
        return (lax.all_gather(shard, TENSOR, axis=0, tiled=True),)
    return (shard, swap(shard, TENSOR, 1), swap(shard, TENSOR, 2))


def gather_finish(hop):
    if lax.axis_size(TENSOR) != 4:
        return hop[0]
    shard, first, second = hop
    half = shard.shape[0] // 2
    top = swap(second[:half], TENSOR, 1)
    bottom = swap(first[half:], TENSOR, 2)
    return jnp.concatenate([shard, first, second, top, bottom])


def add(left, right):
    return (left.astype(F32) + right.astype(F32)).astype(BF16)


def reduce_start(share):
    if lax.axis_size(TENSOR) != 4:
        return (share,)
    rows = share.shape[0] // 4
    own, first, second, far = [share[k * rows : (k + 1) * rows] for k in range(4)]
    half = rows // 2
    return (own, first, second, swap(far[:half], TENSOR, 1), swap(far[half:], TENSOR, 2))


def reduce_middle(hop):
    if lax.axis_size(TENSOR) != 4:
        return hop
    own, first, second, top, bottom = hop
    half = top.shape[0]
    return (
        own,
        jnp.concatenate([first[:half], add(first[half:], bottom)]),
        jnp.concatenate([add(second[:half], top), second[half:]]),
    )


def reduce_finish(hop):
    if lax.axis_size(TENSOR) != 4:
        return lax.psum_scatter(hop[0], TENSOR, scatter_dimension=0, tiled=True).astype(F32)
    own, to_first, to_second = hop
    from_first = swap(to_first, TENSOR, 1)
    from_second = swap(to_second, TENSOR, 2)
    return own.astype(F32) + from_first.astype(F32) + from_second.astype(F32)


def rope(value, cosine, sine):
    return value * cosine + pltpu.roll(value, HEAD_SIZE // 2, 1) * sine


def unrope(value, cosine, sine):
    return value * cosine - pltpu.roll(value, HEAD_SIZE // 2, 1) * sine


def dot(left, right, left_dim, right_dim):
    return lax.dot_general(
        left, right, (((left_dim,), (right_dim,)), ((), ())), preferred_element_type=F32
    )


def lane_column(block, lane):
    lanes = lax.broadcasted_iota(jnp.int32, block.shape, 1)
    return jnp.sum(jnp.where(lanes == lane, block, 0.0), axis=-1, keepdims=True)


def tile_visibility(ids_ref, prefix, query_slot, key_slot, rows):
    query_piece = ids_ref[query_slot]
    key_piece = ids_ref[key_slot]
    full = jnp.logical_or(key_piece < query_piece, (key_piece + 1) * rows <= prefix)
    some = jnp.logical_or(key_piece == query_piece, key_piece * rows < prefix)
    return full, jnp.logical_and(some, jnp.logical_not(full)), query_piece * rows, key_piece * rows


def allowed_tile(shape, rows, query_start, key_start, prefix):
    query = lax.rem(lax.broadcasted_iota(jnp.int32, shape, 0), rows) + query_start
    key = lax.broadcasted_iota(jnp.int32, shape, 1) + key_start
    return jnp.logical_or(key <= query, key < prefix)


SCORE_SCALE = HEAD_SIZE ** (-0.5)
LOG2_SCALE = SCORE_SCALE * math.log2(math.e)


def forward_body(
    ids_ref, prefix_ref, q_ref, k_ref, v_ref, gate_ref, cos_q, sin_q, cos_k, sin_k, gain_q, gain_k,
    gated_ref, mixed_ref, log_ref, key_scr, value_scr, sum_scr,
):
    kv_head, slot = pl.program_id(0), pl.program_id(1)
    rows = q_ref.shape[0]
    slots = k_ref.shape[0] // rows
    group = q_ref.shape[1] // HEAD_SIZE
    prefix = prefix_ref[0]

    @pl.when(slot == 0)
    def _():
        key_scr[...] = rope(scaled_norm(k_ref[...], gain_k[...]), cos_k[...], sin_k[...]).astype(BF16)
        value_scr[:, :HEAD_SIZE] = v_ref[...].astype(BF16)
        value_scr[:, HEAD_SIZE:] = jnp.ones_like(value_scr[:, HEAD_SIZE:])

    query = jnp.concatenate(
        [
            rope(
                scaled_norm(q_ref[:, h * HEAD_SIZE : (h + 1) * HEAD_SIZE], gain_q[...]),
                cos_q[...],
                sin_q[...],
            ).astype(BF16)
            for h in range(group)
        ]
    )
    sum_scr[...] = jnp.zeros_like(sum_scr)

    for key_slot in range(slots):
        full, partial, query_start, key_start = tile_visibility(
            ids_ref, prefix, slot, key_slot, rows
        )
        tile = slice(key_slot * rows, (key_slot + 1) * rows)

        def step(masked):
            expo = jnp.exp2(dot(query, key_scr[tile, :], 1, 1) * LOG2_SCALE)
            if masked:
                expo = jnp.where(
                    allowed_tile(expo.shape, rows, query_start, key_start, prefix), expo, 0.0
                )
            sum_scr[...] += dot(expo.astype(BF16), value_scr[tile, :], 1, 0)

        pl.when(full)(functools.partial(step, False))
        pl.when(partial)(functools.partial(step, True))

    gate = jax.nn.sigmoid(gate_ref[...])
    for h in range(group):
        part = slice(h * rows, (h + 1) * rows)
        columns = slice(h * HEAD_SIZE, (h + 1) * HEAD_SIZE)
        total = sum_scr[part, HEAD_SIZE:]
        mixed = sum_scr[part, :HEAD_SIZE] / total
        mixed_ref[:, columns] = mixed
        log_ref[:, columns] = jnp.log2(total)
        gated_ref[:, columns] = (mixed * lane_column(gate, kv_head * group + h)).astype(BF16)


def head_norm_backward(value, gain, grad):
    inverse = inverse_rms(value)
    weighted = grad * gain
    centre = jnp.mean(weighted * value, axis=-1, keepdims=True)
    return (
        inverse * (weighted - value * (inverse * inverse * centre)),
        jnp.sum(grad * value * inverse, axis=0, keepdims=True),
    )


def backward_body(
    ids_ref, prefix_ref, q_ref, k_ref, v_ref, gate_ref, cos_q, sin_q, cos_k, sin_k, gain_q, gain_k,
    grad_ref, mixed_ref, log_ref,
    joint_ref, gains_ref, key_scr, value_scr, grad_key_scr, grad_value_scr, grad_query_scr, gate_scr,
    gain_scr,
):
    kv_head, slot = pl.program_id(0), pl.program_id(1)
    rows = q_ref.shape[0]
    slots = k_ref.shape[0] // rows
    group = q_ref.shape[1] // HEAD_SIZE
    kv_heads = pl.num_programs(0)
    prefix = prefix_ref[0]

    @pl.when(jnp.logical_and(slot == 0, kv_head == 0))
    def _():
        gate_scr[...] = jnp.zeros_like(gate_scr)
        gain_scr[...] = jnp.zeros_like(gain_scr)

    @pl.when(slot == 0)
    def _():
        key_scr[...] = rope(scaled_norm(k_ref[...], gain_k[...]), cos_k[...], sin_k[...]).astype(BF16)
        value_scr[...] = v_ref[...].astype(BF16)
        grad_key_scr[...] = jnp.zeros_like(grad_key_scr)
        grad_value_scr[...] = jnp.zeros_like(grad_value_scr)

    row_start = pl.multiple_of(slot * rows, rows)
    gate = jax.nn.sigmoid(gate_ref[...])
    lanes = lax.broadcasted_iota(jnp.int32, gate.shape, 1)
    query, mixed_grad, centre = [], [], []
    gate_grad = jnp.zeros_like(gate)
    for h in range(group):
        columns = slice(h * HEAD_SIZE, (h + 1) * HEAD_SIZE)
        query.append(
            rope(scaled_norm(q_ref[:, columns], gain_q[...]), cos_q[...], sin_q[...]).astype(BF16)
        )
        head_gate = lane_column(gate, kv_head * group + h)
        grad = grad_ref[:, columns]
        product = jnp.sum(grad * mixed_ref[:, columns], axis=-1, keepdims=True)
        gate_grad = gate_grad + jnp.where(
            lanes == kv_head * group + h, product * head_gate * (1.0 - head_gate), 0.0
        )
        low = (grad * head_gate).astype(BF16)
        mixed_grad.append(low)
        centre.append(
            jnp.sum(low.astype(F32) * mixed_ref[:, columns], axis=-1, keepdims=True)
        )
    gate_scr[pl.ds(row_start, rows), :] += gate_grad
    query = jnp.concatenate(query)
    mixed_grad = jnp.concatenate(mixed_grad)
    centre = jnp.concatenate(centre)
    logs = jnp.concatenate(
        [log_ref[:, h * HEAD_SIZE : h * HEAD_SIZE + 1] for h in range(group)]
    )
    grad_query_scr[...] = jnp.zeros_like(grad_query_scr)

    for key_slot in range(slots):
        full, partial, query_start, key_start = tile_visibility(
            ids_ref, prefix, slot, key_slot, rows
        )
        tile = slice(key_slot * rows, (key_slot + 1) * rows)

        def step(masked):
            probs = jnp.exp2(dot(query, key_scr[tile, :], 1, 1) * LOG2_SCALE - logs)
            if masked:
                probs = jnp.where(
                    allowed_tile(probs.shape, rows, query_start, key_start, prefix), probs, 0.0
                )
            grad_probs = dot(mixed_grad, value_scr[tile, :], 1, 1)
            grad_scores = (probs * (grad_probs - centre)).astype(BF16)
            grad_query_scr[...] += dot(grad_scores, key_scr[tile, :], 1, 0)
            grad_key_scr[tile, :] += dot(grad_scores, query, 0, 0)
            grad_value_scr[tile, :] += dot(probs.astype(BF16), mixed_grad, 0, 0)

        pl.when(full)(functools.partial(step, False))
        pl.when(partial)(functools.partial(step, True))

    for h in range(group):
        columns = slice(h * HEAD_SIZE, (h + 1) * HEAD_SIZE)
        grad = unrope(
            grad_query_scr[h * rows : (h + 1) * rows, :] * SCORE_SCALE, cos_q[...], sin_q[...]
        )
        value, term = head_norm_backward(q_ref[:, columns], gain_q[...], grad)
        gain_scr[0:1, :] += term
        start = pl.multiple_of((kv_head * group + h) * HEAD_SIZE, HEAD_SIZE)
        joint_ref[pl.ds(row_start, rows), pl.ds(start, HEAD_SIZE)] = value.astype(BF16)

    @pl.when(slot == slots - 1)
    def _():
        grad = unrope(grad_key_scr[...] * SCORE_SCALE, cos_k[...], sin_k[...])
        value, term = head_norm_backward(k_ref[...], gain_k[...], grad)
        gain_scr[1:2, :] += term
        start = pl.multiple_of((kv_heads * group + kv_head) * HEAD_SIZE, HEAD_SIZE)
        joint_ref[:, pl.ds(start, HEAD_SIZE)] = value.astype(BF16)
        start = pl.multiple_of((kv_heads * (group + 1) + kv_head) * HEAD_SIZE, HEAD_SIZE)
        joint_ref[:, pl.ds(start, HEAD_SIZE)] = grad_value_scr[...].astype(BF16)

    @pl.when(jnp.logical_and(slot == slots - 1, kv_head == kv_heads - 1))
    def _():
        joint_ref[:, joint_ref.shape[1] - LANES :] = gate_scr[...].astype(BF16)
        gains_ref[...] = gain_scr[...]


def attention_specs(span, slots, heads, kv_heads):
    rows = span // slots
    group = heads // kv_heads
    whole = lambda column: pl.BlockSpec((span, HEAD_SIZE), lambda g, i, *_: (0, column(g)))
    return [
        pl.BlockSpec((rows, group * HEAD_SIZE), lambda g, i, *_: (i, g)),
        whole(lambda g: heads + g),
        whole(lambda g: heads + kv_heads + g),
        pl.BlockSpec((rows, LANES), lambda g, i, *_: (i, heads + 2 * kv_heads)),
        pl.BlockSpec((rows, HEAD_SIZE), lambda g, i, *_: (i, 0)),
        pl.BlockSpec((rows, HEAD_SIZE), lambda g, i, *_: (i, 0)),
        whole(lambda g: 0),
        whole(lambda g: 0),
        pl.BlockSpec((1, HEAD_SIZE), lambda g, i, *_: (0, 0)),
        pl.BlockSpec((1, HEAD_SIZE), lambda g, i, *_: (0, 0)),
    ]


def attention_forward(ids, prefix, joint, cosine, sine, gain_q, gain_k, heads, kv_heads):
    span, slots = joint.shape[0], ids.shape[0]
    rows, group = span // slots, heads // kv_heads
    block = pl.BlockSpec((rows, group * HEAD_SIZE), lambda g, i, *_: (i, g))
    return pl.pallas_call(
        forward_body,
        grid_spec=pltpu.PrefetchScalarGridSpec(
            num_scalar_prefetch=2,
            grid=(kv_heads, slots),
            in_specs=attention_specs(span, slots, heads, kv_heads),
            out_specs=[block, block, block],
            scratch_shapes=[
                pltpu.VMEM((span, HEAD_SIZE), BF16),
                pltpu.VMEM((span, 2 * HEAD_SIZE), BF16),
                pltpu.VMEM((group * rows, 2 * HEAD_SIZE), F32),
            ],
        ),
        out_shape=[
            jax.ShapeDtypeStruct((span, heads * HEAD_SIZE), BF16),
            jax.ShapeDtypeStruct((span, heads * HEAD_SIZE), F32),
            jax.ShapeDtypeStruct((span, heads * HEAD_SIZE), F32),
        ],
        cost_estimate=pl.CostEstimate(
            flops=3 * heads * span * span * HEAD_SIZE,
            bytes_accessed=joint.size * 4 + span * heads * HEAD_SIZE * 10,
            transcendentals=heads * span * span,
        ),
        name="attention_forward",
    )(ids, prefix, joint, joint, joint, joint, cosine, sine, cosine, sine, gain_q, gain_k)


def attention_backward(
    ids, prefix, joint, cosine, sine, gain_q, gain_k, grad, mixed, logs, heads, kv_heads
):
    span, slots = joint.shape[0], ids.shape[0]
    rows, group = span // slots, heads // kv_heads
    block = pl.BlockSpec((rows, group * HEAD_SIZE), lambda g, i, *_: (i, g))
    return pl.pallas_call(
        backward_body,
        grid_spec=pltpu.PrefetchScalarGridSpec(
            num_scalar_prefetch=2,
            grid=(kv_heads, slots),
            in_specs=attention_specs(span, slots, heads, kv_heads) + [block, block, block],
            out_specs=[
                pl.BlockSpec(joint.shape, lambda g, i, *_: (0, 0)),
                pl.BlockSpec((8, HEAD_SIZE), lambda g, i, *_: (0, 0)),
            ],
            scratch_shapes=[
                pltpu.VMEM((span, HEAD_SIZE), BF16),
                pltpu.VMEM((span, HEAD_SIZE), BF16),
                pltpu.VMEM((span, HEAD_SIZE), F32),
                pltpu.VMEM((span, HEAD_SIZE), F32),
                pltpu.VMEM((group * rows, HEAD_SIZE), F32),
                pltpu.VMEM((span, LANES), F32),
                pltpu.VMEM((8, HEAD_SIZE), F32),
            ],
        ),
        out_shape=[
            jax.ShapeDtypeStruct(joint.shape, BF16),
            jax.ShapeDtypeStruct((8, HEAD_SIZE), F32),
        ],
        cost_estimate=pl.CostEstimate(
            flops=8 * heads * span * span * HEAD_SIZE,
            bytes_accessed=joint.size * 6 + span * heads * HEAD_SIZE * 12,
            transcendentals=heads * span * span,
        ),
        name="attention_backward",
    )(
        ids, prefix, joint, joint, joint, joint, cosine, sine, cosine, sine, gain_q, gain_k,
        grad, mixed, logs,
    )


def middle_body(joint_ref, cotangent_ref, down_ref, hidden_ref, grad_ref):
    width = hidden_ref.shape[1]
    chunk = min(256, hidden_ref.shape[0])
    for start in range(0, hidden_ref.shape[0], chunk):
        rows = slice(start, start + chunk)
        grad = dot(cotangent_ref[rows, :], down_ref[...], 1, 1)
        gate = joint_ref[rows, :width]
        up = joint_ref[rows, width:]
        sigmoid = jax.nn.sigmoid(gate)
        silu = gate * sigmoid
        hidden_ref[rows, :] = (silu * up).astype(BF16)
        grad_ref[rows, :width] = (grad * up * (sigmoid * (1.0 + gate * (1.0 - sigmoid)))).astype(BF16)
        grad_ref[rows, width:] = (grad * silu).astype(BF16)


def feedforward_middle(joint, cotangent, down, block):
    span, hidden, width = joint.shape[0], down.shape[0], down.shape[1]
    return pl.pallas_call(
        middle_body,
        grid=(hidden // block,),
        in_specs=[
            pl.BlockSpec((span, 2 * block), lambda h: (0, h)),
            pl.BlockSpec((span, width), lambda h: (0, 0)),
            pl.BlockSpec((block, width), lambda h: (h, 0)),
        ],
        out_specs=[
            pl.BlockSpec((span, block), lambda h: (0, h)),
            pl.BlockSpec((span, 2 * block), lambda h: (0, h)),
        ],
        out_shape=[
            jax.ShapeDtypeStruct((span, hidden), BF16),
            jax.ShapeDtypeStruct((span, 2 * hidden), BF16),
        ],
        cost_estimate=pl.CostEstimate(
            flops=2 * span * hidden * width,
            bytes_accessed=joint.size * 6 + cotangent.size * 2 + down.size * 2,
            transcendentals=span * hidden,
        ),
        name="feedforward_middle",
    )(joint, cotangent, down)


def interleave(left, right, block):
    parts = []
    for start in range(0, left.shape[1], block):
        parts += [left[:, start : start + block], right[:, start : start + block]]
    return jnp.concatenate(parts, axis=1)


def separate(value, block):
    take = lambda first: jnp.concatenate(
        [value[:, k : k + block] for k in range(first, value.shape[1], 2 * block)], axis=1
    )
    return take(0), take(block)


def on_device(
    layer_input,
    prefix_lengths,
    gains,
    w_query,
    key_matrix,
    value_matrix,
    w_gate_head,
    w_output,
    w_gate,
    w_up,
    w_down,
    out_grad,
):
    sequences = range(layer_input.shape[0])
    size = lax.axis_size(TENSOR)
    rows = layer_input.shape[1]
    width = layer_input.shape[2]
    query_columns = w_query.shape[1]
    key_columns = key_matrix.shape[1]
    heads = query_columns // HEAD_SIZE
    kv_heads = key_columns // HEAD_SIZE

    all_gains = small_gather(small_gather(gains, DP), TENSOR)
    all_gains = all_gains.reshape(size, -1, gains.shape[0]).swapaxes(0, 1).reshape(-1)
    gain_attn = all_gains[:width]
    gain_ffn = all_gains[width : 2 * width]
    gain_query = all_gains[2 * width : 2 * width + HEAD_SIZE].reshape(1, -1)
    key_norm_gain = all_gains[2 * width + HEAD_SIZE :].reshape(1, -1)

    padded_gate = jnp.pad(w_gate_head, ((0, 0), (0, LANES - w_gate_head.shape[1])))
    block = math.gcd(256, w_gate.shape[1])
    w_joint = lax.all_gather(
        jnp.concatenate([w_query, key_matrix, value_matrix, padded_gate], axis=1),
        DP,
        axis=0,
        tiled=True,
    )
    output_w = lax.all_gather(w_output, DP, axis=1, tiled=True)
    both_w = lax.all_gather(interleave(w_gate, w_up, block), DP, axis=0, tiled=True)
    down_w = lax.all_gather(w_down, DP, axis=1, tiled=True)

    ids = piece_ids()
    positions = (ids[:, None] * rows + jnp.arange(rows, dtype=jnp.int32)[None, :]).reshape(-1)
    cosine_table, sine_table = rope_tables(positions)
    barrier = lax.optimization_barrier

    def scatter(value, dim):
        shard = lax.psum_scatter(value, DP, scatter_dimension=dim, tiled=True)
        return shard.astype(F32)


    late = lambda value, after: barrier((value, after))[0]
    inputs = [barrier(layer_input[s]) for s in sequences]
    grads = [barrier(out_grad[s]) for s in sequences]
    x_rows = [inputs[s].astype(F32) for s in sequences]
    inverses = [barrier(inverse_rms(x_rows[s])) for s in sequences]
    cotangent = [gather_finish(gather_start(grads[s])) for s in sequences]
    whole = [gather_finish(gather_start(inputs[s])) for s in sequences]

    joints, gated, mixed, logs, middle, ffn_low, normed_ffn = [], [], [], [], [], [], []
    normed = []
    hops, ffn_inverses = [], []
    for s in sequences:
        gain_now = gain_attn if s == 0 else late(gain_attn, joints[s - 1])
        normed.append(barrier(scaled_norm(barrier(whole[s]).astype(F32), gain_now).astype(BF16)))
        joints.append(matmul(normed[s], w_joint))
        outs = attention_forward(
            ids, prefix_lengths[s : s + 1], joints[s], cosine_table, sine_table, gain_query,
            key_norm_gain, heads, kv_heads,
        )
        for kept, out in zip((gated, mixed, logs), outs):
            kept.append(out)
        share = matmul(gated[s], output_w).astype(BF16)
        hops.append(reduce_middle(reduce_start(share)))
    opened = ()
    for s in sequences:
        hop = hops[s]
        x_late, gain_late = late((inputs[s], gain_ffn), (hop, opened, ffn_low))
        middle.append(barrier(x_late.astype(F32) + reduce_finish(hop)))
        ffn_inverses.append(barrier(inverse_rms(middle[s])))
        ffn_low.append(barrier((middle[s] * ffn_inverses[s] * gain_late).astype(BF16)))
        opened = gather_start(ffn_low[s])
        normed_ffn.append(gather_finish(opened))

    hidden, grad_both, grad_middle, gain_ffn_terms, branch = [], [], [], [], []
    hops = []
    for s in sequences:
        gate_up = matmul(normed_ffn[s], both_w)
        outs = feedforward_middle(gate_up, cotangent[s], down_w, block)
        hidden.append(outs[0])
        grad_both.append(outs[1])
        share = right_product(grad_both[s], both_w).astype(BF16)
        hops.append(reduce_middle(reduce_start(share)))
    for s in sequences:
        hop = hops[s]
        middle_late, inverse_late, grad_late, gain_late = late(
            (middle[s], ffn_inverses[s], grads[s], gain_ffn), (hop, grad_middle)
        )
        term, gain_term = norm_backward(middle_late, inverse_late, gain_late, reduce_finish(hop))
        gain_ffn_terms.append(barrier(gain_term))
        grad_middle.append(barrier(term + grad_late.astype(F32)))
        hop = gather_start(grad_middle[s].astype(BF16))
        branch.append(gather_finish(hop))

    def weight_grad(left, right):
        total = left_product(left[0], right[0])
        for s in sequences[1:]:
            total = left_product(left[s], late(right[s], total)) + total
        return total.astype(BF16)

    out_down = scatter(weight_grad(hidden, cotangent), 1)
    out_both = scatter(weight_grad(normed_ffn, grad_both), 0)

    joint_grads, head_gain_terms, blocks, input_rows, gain_attn_terms = [], [], [], [], []
    hops, out_hops = [], []
    for s in sequences:
        share = matmul(hidden[s], down_w).astype(BF16)
        out_hops.append(reduce_middle(reduce_start(share)))
        grad_gated = right_product(branch[s], output_w)
        joint_grad, head_gains = attention_backward(
            ids, prefix_lengths[s : s + 1], joints[s], cosine_table, sine_table, gain_query,
            key_norm_gain, grad_gated, mixed[s], logs[s], heads, kv_heads,
        )
        joint_grads.append(joint_grad)
        head_gain_terms.append(head_gains[:2].reshape(-1))
        share = right_product(joint_grads[s], w_joint).astype(BF16)
        hops.append(reduce_middle(reduce_start(share)))
    out_output = scatter(weight_grad(gated, branch), 1)
    out_gate, out_up = separate(out_both, block)
    finished = (out_down, out_gate, out_up, out_output)
    for s in sequences:
        hop = hops[s]
        before = (hop, hops[-1], input_rows) + (finished if s == sequences[-1] else ())
        x_late, inverse_late, grad_late, gain_late = late(
            (inputs[s], inverses[s], grad_middle[s], gain_attn), before
        )
        grad_rows, gain_term = norm_backward(
            x_late.astype(F32), inverse_late, gain_late, reduce_finish(hop)
        )
        gain_attn_terms.append(barrier(gain_term))
        input_rows.append(barrier(grad_late + grad_rows))
    for s in sequences:
        hop = out_hops[s]
        middle_late = late(middle[s], (hop, gain_attn_terms))
        blocks.append(barrier((middle_late + reduce_finish(hop)).astype(BF16)))
    out_joint = scatter(weight_grad(normed, joint_grads), 0)
    total = lambda terms: sum(terms[1:], terms[0])
    gain_total = jnp.concatenate(
        [total(gain_attn_terms), total(gain_ffn_terms), total(head_gain_terms)]
    )
    gains_grad = small_scatter(small_scatter(gain_total, DP), TENSOR)
    value_start = query_columns + key_columns
    gate_start = value_start + key_columns
    return (
        jnp.stack(blocks),
        jnp.stack(input_rows),
        gains_grad,
        out_joint[:, :query_columns],
        out_joint[:, query_columns:value_start],
        out_joint[:, value_start:gate_start],
        out_joint[:, gate_start : gate_start + heads],
        out_output,
        out_gate,
        out_up,
        out_down,
    )


def solution(mesh):
    rows = P(DP, TENSOR, None)
    gain = P((DP, TENSOR))
    into, out_of = P(DP, TENSOR), P(TENSOR, DP)
    weights = (into, into, into, into, out_of, into, into, out_of)

    return jax.shard_map(
        on_device,
        mesh=mesh,
        in_specs=(rows, P(DP), gain) + weights + (rows,),
        out_specs=(rows, rows, gain) + weights,
        check_vma=False,
    )
```
